512 devices in a mesh: kpt: 16 (over x, y_hi), occ: 32 (over y_lo, z, core).
Axes of the slice: x: 4, y: 8 (y_hi: 4, y_lo: 2; y = y_hi * 2 + y_lo), z: 8, core: 2. Of those that a mesh axis runs over, the one named last changes fastest.
Arguments:
- factor: bfloat16 [2, 32, 32, 2, 256, 512], P(None, 'kpt', 'occ'), may hold values from -1.0546875 to 1.0546875
- partner: int32 [2, 32], replicated, may hold values from 0 to 31, as said below
- occ_energy: float32 [32, 32], replicated, may hold values from -3 to -0.5
- vir_sorted: float32 [32, 256], replicated, may hold values from 0.3 to 4.3, as said below
- vir_order: int32 [32, 256], replicated, may hold values from 0 to 255, each once within a row
Outputs:
- gradient_factor: bfloat16 [2, 32, 32, 2, 256, 512], P(None, 'kpt', 'occ')
The draws below stay inside these ranges and needn't reach their ends.
Inputs may be any that keep to these rules, and one draw needn't show every extreme that they name: With group g holding k-points g * 2 to (g + 1) * 2 - 1, partner[0, k] lies in group (k // 2) XOR 1 and partner[1, k] in group (k // 2) XOR 8; which k-point of that group is arbitrary, and several k-points may share one. `vir_sorted`: each row is ascending and begins with 0.3.
All inputs are finite; a program needn't handle non-finite values.
Results may differ from the reference program's by a relative error of at most 0.0037.
Values may be sent and summed in bfloat16 or wider, within the bound.
A program may use at most 64 MiB of HBM per device.

```python
from functools import partial
import jax
import jax.numpy as jnp
from jax import lax

NV = 256
NAUX = 512
K_DEV = 2
NTR = 2
REACH = 1
NK = 32
NOCC = 32


def draw_partner(key, part):
    groups = NK // K_DEV
    point_ids = jnp.arange(NK, dtype=jnp.int32)
    group_of = point_ids // K_DEV
    first_slot = jnp.remainder(point_ids, K_DEV) == 0
    tables = []
    for transfer in range(NTR):
        flip_mask = 1 if transfer == 0 else groups // 2
        other_group = jnp.bitwise_xor(group_of, flip_mask)
        slots = jax.random.randint(jax.random.fold_in(key, 71 + transfer), (NK,), 0, K_DEV).astype(jnp.int32)
        if transfer == 1:
            to_last = jnp.logical_and(first_slot, group_of == groups // 2 - 1)
            to_first = jnp.logical_and(first_slot, group_of == groups // 2)
            slots = jnp.where(to_last, K_DEV - 1, slots)
            slots = jnp.where(to_first, 0, slots)
        table = other_group * K_DEV + slots
        tables.append(table.astype(jnp.int32))
    return jnp.stack(tables, axis=0)


def draw_vir_sorted(key, part):
    uniform_part = jax.random.uniform(jax.random.fold_in(key, 313), (NK, NV), jnp.float32)
    increments = 4.0 / NV * uniform_part
    running = jnp.cumsum(increments, axis=1)
    return (0.3 + running - running[:, 0:1]).astype(jnp.float32)


def levels(stream_key, extent, pieces, least, high):
    gain = 1.0
    for axis_at, blocks in pieces:
        draws = jax.random.uniform(jax.random.fold_in(jax.random.fold_in(stream_key, 6), axis_at), (blocks,), jnp.float32, least / len(pieces), high / len(pieces))
        gain = gain * jnp.repeat(jnp.exp(draws), extent[axis_at] // blocks).reshape((-1,) + (1,) * (len(extent) - 1 - axis_at))
    return gain


def normal_values(rng, dims, width, reach, pieces=(), kind=jnp.bfloat16):
    factor_of = levels(rng, dims, pieces, -0.22, 0.18) if pieces else 1.0
    result = jax.random.normal(rng, dims, jnp.float32) * width * factor_of
    return jnp.minimum(jnp.maximum(result, -reach), reach).astype(kind)


def setup_inputs(seed: int = 0) -> dict:
    key_list = jax.random.split(jax.random.key(seed), 6)
    factor = normal_values(key_list[0], (NTR, NK, NOCC, 2, NV, NAUX), ((2 * NAUX) ** -0.25), 1.0546875, ((1, 16), (2, 32)))
    partner = draw_partner(jax.random.fold_in(key_list[5], 71), 0)
    occ_energy = jnp.clip(jax.random.uniform(key_list[2], (NK, NOCC), jnp.float32, -3.0, -0.5), -3.0, -0.5)
    vir_sorted = draw_vir_sorted(jax.random.fold_in(key_list[5], 71), 0)
    vir_order = jax.vmap(lambda own: jax.random.permutation(own, NV))(jax.random.split(key_list[4], NK)).reshape((NK, NV)).astype(jnp.int32)
    return dict(factor=factor, partner=partner, occ_energy=occ_energy, vir_sorted=vir_sorted, vir_order=vir_order)


def virtual_energies(vir_sorted, vir_order):
    return jnp.take_along_axis(vir_sorted, vir_order, axis=1)


def point_gradient(factor_set, partner_row, occ_energy, virtual, point_id):
    partner_id = partner_row[point_id]
    own_block = factor_set[point_id].astype(jnp.float32)
    far_block = factor_set[partner_id].astype(jnp.float32)
    rotated = jnp.stack([own_block[:, 1], -own_block[:, 0]], axis=1)
    stacked = jnp.stack([own_block, rotated], axis=1)
    gradient = jnp.zeros(own_block.shape, jnp.float32)
    for offset in range(-REACH, REACH + 1):
        window = jnp.roll(far_block, -offset, axis=0)
        pair_ints = jnp.einsum("ircaq,icbq->irab", stacked, window)
        far_occ = jnp.roll(occ_energy[partner_id], -offset)
        denominator = occ_energy[point_id][:, None, None] + far_occ[:, None, None] - virtual[partner_id][None, :, None] - virtual[point_id][None, None, :]
        rounded = (pair_ints / denominator[:, None]).astype(jnp.bfloat16)
        amplitude = lax.optimization_barrier(rounded).astype(jnp.float32)
        real_part = amplitude[:, 0]
        imag_part = amplitude[:, 1]
        combined = jnp.stack([jnp.stack([real_part, -imag_part], axis=1), jnp.stack([imag_part, real_part], axis=1)], axis=1)
        gradient = gradient + jnp.einsum("ixcab,icbq->ixaq", combined, window)
    return gradient.astype(jnp.bfloat16)


def reference(factor, partner, occ_energy, vir_sorted, vir_order):
    virtual = virtual_energies(vir_sorted, vir_order)
    outputs = []
    for transfer in range(NTR):
        worker = partial(point_gradient, factor[transfer], partner[transfer], occ_energy, virtual)
        gradients = lax.map(worker, jnp.arange(NK, dtype=jnp.int32))
        outputs.append(gradients)
    return jnp.stack(outputs, axis=0)
```

```python
import functools

import jax
import jax.numpy as jnp
from jax import lax
from jax.experimental import pallas as pl
from jax.experimental.pallas import tpu as pltpu
from jax.sharding import PartitionSpec as P

MESH = pl.DeviceIdType.MESH
scope = jax.named_scope
NT_DIMS = (((1,), (1,)), ((), ()))

UNIT = 128
CHUNKS = (
    ((0, 32), (32, 32), (64, 32), (96, 32), (128, 32), (160, 32), (192, 32), (224, 16), (240, 16)),
    ((0, 64), (64, 64), (128, 64), (192, 64)),
)
MOST = max(len(chunks) for chunks in CHUNKS)


def kernel(flips, factor_ref, partner_ref, occ_ref, sorted_ref, order_ref, out_ref, *scratch):
    nv = factor_ref.shape[4]
    naux = factor_ref.shape[5]
    halves = nv // UNIT
    windows = scratch[: 2 * halves * 3]
    (own, total, inverse, occ_s, partner_s, sorted_v, order_v,
     send_sems, recv_sems, own_sems, table_sems) = scratch[2 * halves * 3 :]
    window = lambda t, h, role: windows[(t * halves + h) * 3 + role]

    group = lax.axis_index("kpt")
    orbit = lax.axis_index("occ")
    orbits = lax.axis_size("occ")
    odd = lax.rem(orbit, 2)
    near = orbit + 1 - 2 * odd
    far = lax.rem(orbit + orbits - 1 + 2 * odd, orbits)
    partners = [(lax.bitwise_xor(group, 1 << flip), orbit) for flip in flips]
    early = lax.rem(group, 2) != orbit // (orbits // 2)
    near_id = (group, near)
    far_id = (group, far)

    tables = [
        pltpu.make_async_copy(src, dst, table_sems.at[n])
        for n, (src, dst) in enumerate(
            ((partner_ref, partner_s), (occ_ref, occ_s), (sorted_ref, sorted_v), (order_ref, order_v))
        )
    ]
    for copy in tables:
        copy.start()
    owns = []
    for t in (1, 0):
        for k in range(2):
            for n, (c, row, col) in enumerate(((0, 0, 0), (1, 0, 1), (1, 1, 0))):
                owns.append(
                    pltpu.make_async_copy(
                        factor_ref.at[t, k, 0, c],
                        own.at[t, k, pl.ds(row * nv, nv), pl.ds(col * naux, naux)],
                        own_sems.at[t, k, n],
                    )
                )
    for copy in owns:
        copy.start()

    half = orbits // 2
    bent = orbit // half != far // half
    bent_id = (partners[1][0], far)

    barrier = pltpu.get_barrier_semaphore()
    for target in (*partners, near_id, far_id):
        pl.semaphore_signal(barrier, inc=1, device_id=target, device_id_type=MESH)

    @pl.when(bent)
    def _():
        pl.semaphore_signal(barrier, inc=1, device_id=bent_id, device_id_type=MESH)

    with scope("barrier"):
        pl.semaphore_wait(barrier, 4 + bent.astype(jnp.int32))

    swaps, forwards = {}, {}
    for c in range(MOST):
        for t in range(2):
            if c < len(CHUNKS[t]):
                row, rows = CHUNKS[t][c]
                h, at = row // UNIT, row % UNIT
                here = window(t, h, 0).at[:, :, pl.ds(at, rows), :]
                swaps[t, c] = pltpu.make_async_remote_copy(
                    src_ref=factor_ref.at[t, :, 0, :, pl.ds(row, rows), :],
                    dst_ref=here,
                    send_sem=send_sems.at[0, t, c],
                    recv_sem=recv_sems.at[0, t, c],
                    device_id=partners[t],
                    device_id_type=MESH,
                )
                if t == 1:
                    straight = pltpu.make_async_remote_copy(
                        src_ref=factor_ref.at[t, :, 0, :, pl.ds(row, rows), :],
                        dst_ref=window(t, h, 2).at[:, :, pl.ds(at, rows), :],
                        send_sem=send_sems.at[2, t, c],
                        recv_sem=recv_sems.at[2, t, c],
                        device_id=bent_id,
                        device_id_type=MESH,
                    )
                    pl.when(bent)(straight.start)
                swaps[t, c].start()
                for role, target in ((2, far_id), (1, near_id)):
                    forwards[t, c, role] = pltpu.make_async_remote_copy(
                        src_ref=here,
                        dst_ref=window(t, h, role).at[:, :, pl.ds(at, rows), :],
                        send_sem=send_sems.at[role, t, c],
                        recv_sem=recv_sems.at[role, t, c],
                        device_id=target,
                        device_id_type=MESH,
                    )

    def take(t, *chunks):
        for c in chunks:
            with scope("take%d%d" % (t, c)):
                swaps[t, c].wait_recv()
                if t == 1:
                    pl.when(jnp.logical_not(bent))(forwards[t, c, 2].start)
                else:
                    forwards[t, c, 2].start()
                forwards[t, c, 1].start()

    def arrived(t, h, role):
        with scope("arrive%d%d%d" % (t, h, role)):
            for c, (row, _) in enumerate(CHUNKS[t]):
                if row // UNIT == h:
                    forwards[t, c, role].wait_recv()

    for copy in tables:
        copy.wait()
    for copy in owns:
        copy.wait()
    for t in range(2):
        for k in range(2):
            own[t, k, nv:, naux:] = -own[t, k, :nv, :naux]

    lane = lax.broadcasted_iota(jnp.int32, (nv, nv), 1)
    sub = lax.broadcasted_iota(jnp.int32, (nv, nv), 0)
    same = lane == sub

    def as_column(row, zero):
        return jnp.sum(jnp.where(same, row, zero), axis=1, keepdims=True)

    def virtual_row(k):
        ranks = order_v[pl.ds(k, 1), :]
        levels = as_column(sorted_v[pl.ds(k, 1), :], 0.0)
        return jnp.sum(jnp.where(ranks == sub, levels, 0.0), axis=0, keepdims=True)

    roles = (orbit, near, far)
    for k in range(2):
        own_k = group * 2 + k
        own_virtual = virtual_row(own_k)
        own_occ = occ_s[own_k, orbit]
        for t in range(2):
            point = partner_s[t, own_k]
            far_virtual = as_column(virtual_row(point), 0.0)
            for role in range(3):
                pair_occ = own_occ + occ_s[point, roles[role]]
                inverse[t, k, role] = 1.0 / ((pair_occ - far_virtual) - own_virtual)

    def part(t, h, k, role):
        slot = lax.rem(partner_s[t, group * 2 + k], 2)
        rows = window(t, h, role)[slot]
        side = jnp.concatenate([rows[0], rows[1]], axis=1)
        pair = lax.dot_general(own[t, k], side, NT_DIMS, preferred_element_type=jnp.float32)
        scale = inverse[t, k, role, :, h * UNIT : (h + 1) * UNIT]
        real = (pair[:nv] * scale).astype(jnp.bfloat16)
        imag = (pair[nv:] * scale).astype(jnp.bfloat16)
        mixed = jnp.concatenate(
            [jnp.concatenate([real, -imag], axis=1), jnp.concatenate([imag, real], axis=1)], axis=0
        )
        return mixed, rows.reshape(2 * UNIT, naux)

    def gradient(parts):
        mixed = jnp.concatenate([m for m, _ in parts], axis=1)
        rows = jnp.concatenate([r for _, r in parts], axis=0)
        return jnp.dot(mixed, rows, preferred_element_type=jnp.float32)

    def finish(t, k, value):
        out_ref[t, k, 0, 0] = value[:nv].astype(jnp.bfloat16)
        out_ref[t, k, 0, 1] = value[nv:].astype(jnp.bfloat16)

    def unit(t, h):
        for role in (1, 2):
            arrived(t, h, role)

        with scope("unit%d%d" % (t, h)):

            @pl.loop(0, 2)
            def _(k):
                value = gradient([part(t, h, k, role) for role in range(3)])
                if h == 0:
                    total[t, k] = value
                else:
                    finish(t, k, total[t, k] + value)

    def last(t, h):
        arrived(t, h, 1)
        with scope("near"):

            @pl.loop(0, 2)
            def _(k):
                total[t, k] += gradient([part(t, h, k, role) for role in range(2)])

        arrived(t, h, 2)
        with scope("far"):
            for k in range(2):
                finish(t, k, total[t, k] + gradient([part(t, h, k, 2)]))

    @pl.when(early)
    def _():
        for t, c in ((0, 0), (1, 0), (0, 1), (0, 2), (1, 1), (0, 3), (0, 4), (0, 5), (1, 2), (0, 6), (0, 7), (0, 8)):
            take(t, c)

    @pl.when(jnp.logical_not(early))
    def _():
        take(1, 0, 1, 2)

    unit(1, 0)
    take(1, 3)

    @pl.when(jnp.logical_not(early))
    def _():
        take(0, 0, 1)

    unit(1, 1)

    @pl.when(jnp.logical_not(early))
    def _():
        take(0, 2, 3, 4)

    @pl.when(jnp.logical_not(early) & bent)
    def _():
        take(0, 5, 6, 7, 8)

    unit(0, 0)

    @pl.when(jnp.logical_not(early | bent))
    def _():
        take(0, 5, 6, 7, 8)

    last(0, 1)

    with scope("drain"):
        for copy in (*swaps.values(), *forwards.values()):
            copy.wait_send()


def body(factor, partner, occ_energy, vir_sorted, vir_order):
    transfers, points, _, _, nv, naux = factor.shape
    top_bit = lax.axis_size("kpt").bit_length() - 2
    halves = nv // UNIT
    scratch = [pltpu.VMEM((points, 2, UNIT, naux), jnp.bfloat16)] * (transfers * halves * 3) + [
        pltpu.VMEM((transfers, points, 2 * nv, 2 * naux), jnp.bfloat16),
        pltpu.VMEM((transfers, points, 2 * nv, naux), jnp.float32),
        pltpu.VMEM((transfers, points, 3, nv, nv), jnp.float32),
        pltpu.SMEM(occ_energy.shape, jnp.float32),
        pltpu.SMEM(partner.shape, jnp.int32),
        pltpu.VMEM(vir_sorted.shape, jnp.float32),
        pltpu.VMEM(vir_order.shape, jnp.int32),
        pltpu.SemaphoreType.DMA((3, transfers, MOST)),
        pltpu.SemaphoreType.DMA((3, transfers, MOST)),
        pltpu.SemaphoreType.DMA((transfers, points, 3)),
        pltpu.SemaphoreType.DMA((4,)),
    ]
    return pl.pallas_call(
        functools.partial(kernel, (0, top_bit)),
        out_shape=jax.ShapeDtypeStruct(factor.shape, jnp.bfloat16),
        in_specs=[pl.BlockSpec(memory_space=pltpu.HBM)] * 5,
        out_specs=pl.BlockSpec(memory_space=pltpu.VMEM),
        scratch_shapes=scratch,
        compiler_params=pltpu.CompilerParams(
            collective_id=0, has_side_effects=True, vmem_limit_bytes=40 << 20
        ),
        name="exchange_contract",
    )(*(pltpu.with_memory_space_constraint(x, pltpu.HBM) for x in (factor, partner, occ_energy, vir_sorted, vir_order)))


def solution(mesh):
    in_specs = (P(None, "kpt", "occ", None, None, None), P(), P(), P(), P())
    out_specs = P(None, "kpt", "occ", None, None, None)
    return jax.shard_map(body, mesh=mesh, in_specs=in_specs, out_specs=out_specs, check_vma=False)
```

```python
import functools

import jax
import jax.numpy as jnp
from jax import lax
from jax.experimental import pallas as pl
from jax.experimental.pallas import tpu as pltpu
from jax.sharding import PartitionSpec as P

MESH = pl.DeviceIdType.MESH
scope = jax.named_scope
NT_DIMS = (((1,), (1,)), ((), ()))

UNIT = 128
CHUNKS = (
    ((0, 32), (32, 32), (64, 32), (96, 32), (128, 32), (160, 32), (192, 32), (224, 16), (240, 16)),
    ((0, 64), (64, 64), (128, 64), (192, 64)),
)
MOST = max(len(chunks) for chunks in CHUNKS)


def kernel(flips, factor_ref, partner_ref, occ_ref, sorted_ref, order_ref, out_ref, *scratch):
    nv = factor_ref.shape[4]
    naux = factor_ref.shape[5]
    halves = nv // UNIT
    windows = scratch[: 2 * halves * 3]
    (own, total, inverse, occ_s, partner_s, sorted_v, order_v,
     send_sems, recv_sems, own_sems, table_sems) = scratch[2 * halves * 3 :]
    window = lambda t, h, role: windows[(t * halves + h) * 3 + role]

    group = lax.axis_index("kpt")
    orbit = lax.axis_index("occ")
    orbits = lax.axis_size("occ")
    odd = lax.rem(orbit, 2)
    near = orbit + 1 - 2 * odd
    far = lax.rem(orbit + orbits - 1 + 2 * odd, orbits)
    partners = [(lax.bitwise_xor(group, 1 << flip), orbit) for flip in flips]
    early = lax.rem(group, 2) != orbit // (orbits // 2)
    near_id = (group, near)
    far_id = (group, far)

    tables = [
        pltpu.make_async_copy(src, dst, table_sems.at[n])
        for n, (src, dst) in enumerate(
            ((partner_ref, partner_s), (occ_ref, occ_s), (sorted_ref, sorted_v), (order_ref, order_v))
        )
    ]
    for copy in tables:
        copy.start()
    owns = []
    for t in (1, 0):
        for k in range(2):
            for n, (c, row, col) in enumerate(((0, 0, 0), (1, 0, 1), (1, 1, 0))):
                owns.append(
                    pltpu.make_async_copy(
                        factor_ref.at[t, k, 0, c],
                        own.at[t, k, pl.ds(row * nv, nv), pl.ds(col * naux, naux)],
                        own_sems.at[t, k, n],
                    )
                )
    for copy in owns:
        copy.start()

    half = orbits // 2
    hold = lax.rem(orbit + 2, half) == 0
    bent = orbit // half != far // half
    bent_id = (partners[1][0], far)

    barrier = pltpu.get_barrier_semaphore()
    for target in (*partners, near_id, far_id):
        pl.semaphore_signal(barrier, inc=1, device_id=target, device_id_type=MESH)

    @pl.when(bent)
    def _():
        pl.semaphore_signal(barrier, inc=1, device_id=bent_id, device_id_type=MESH)

    with scope("barrier"):
        pl.semaphore_wait(barrier, 4 + bent.astype(jnp.int32))

    swaps, forwards = {}, {}
    for c in range(MOST):
        for t in range(2):
            if c < len(CHUNKS[t]):
                row, rows = CHUNKS[t][c]
                h, at = row // UNIT, row % UNIT
                here = window(t, h, 0).at[:, :, pl.ds(at, rows), :]
                swaps[t, c] = pltpu.make_async_remote_copy(
                    src_ref=factor_ref.at[t, :, 0, :, pl.ds(row, rows), :],
                    dst_ref=here,
                    send_sem=send_sems.at[0, t, c],
                    recv_sem=recv_sems.at[0, t, c],
                    device_id=partners[t],
                    device_id_type=MESH,
                )
                if t == 1:
                    straight = pltpu.make_async_remote_copy(
                        src_ref=factor_ref.at[t, :, 0, :, pl.ds(row, rows), :],
                        dst_ref=window(t, h, 2).at[:, :, pl.ds(at, rows), :],
                        send_sem=send_sems.at[2, t, c],
                        recv_sem=recv_sems.at[2, t, c],
                        device_id=bent_id,
                        device_id_type=MESH,
                    )
                    pl.when(bent)(straight.start)
                    swaps[t, c].start()
                for role, target in ((2, far_id), (1, near_id)):
                    forwards[t, c, role] = pltpu.make_async_remote_copy(
                        src_ref=here,
                        dst_ref=window(t, h, role).at[:, :, pl.ds(at, rows), :],
                        send_sem=send_sems.at[role, t, c],
                        recv_sem=recv_sems.at[role, t, c],
                        device_id=target,
                        device_id_type=MESH,
                    )

    def send_first_transfer():
        for c in range(len(CHUNKS[0])):
            swaps[0, c].start()

    pl.when(jnp.logical_not(hold))(send_first_transfer)

    def take(t, *chunks):
        for c in chunks:
            with scope("take%d%d" % (t, c)):
                swaps[t, c].wait_recv()
                if t == 1:
                    pl.when(jnp.logical_not(bent))(forwards[t, c, 2].start)
                else:
                    forwards[t, c, 2].start()
                forwards[t, c, 1].start()

    def arrived(t, h, role):
        with scope("arrive%d%d%d" % (t, h, role)):
            for c, (row, _) in enumerate(CHUNKS[t]):
                if row // UNIT == h:
                    forwards[t, c, role].wait_recv()

    for copy in tables:
        copy.wait()
    for copy in owns:
        copy.wait()
    for t in range(2):
        for k in range(2):
            own[t, k, nv:, naux:] = -own[t, k, :nv, :naux]

    lane = lax.broadcasted_iota(jnp.int32, (nv, nv), 1)
    sub = lax.broadcasted_iota(jnp.int32, (nv, nv), 0)
    same = lane == sub

    def as_column(row, zero):
        return jnp.sum(jnp.where(same, row, zero), axis=1, keepdims=True)

    def virtual_row(k):
        ranks = order_v[pl.ds(k, 1), :]
        levels = as_column(sorted_v[pl.ds(k, 1), :], 0.0)
        return jnp.sum(jnp.where(ranks == sub, levels, 0.0), axis=0, keepdims=True)

    roles = (orbit, near, far)
    for k in range(2):
        own_k = group * 2 + k
        own_virtual = virtual_row(own_k)
        own_occ = occ_s[own_k, orbit]
        for t in range(2):
            point = partner_s[t, own_k]
            far_virtual = as_column(virtual_row(point), 0.0)
            for role in range(3):
                pair_occ = own_occ + occ_s[point, roles[role]]
                value = 1.0 / ((pair_occ - far_virtual) - own_virtual)
                for h in range(halves):
                    columns = pl.ds(role * UNIT, UNIT)
                    inverse[t, k, h, :, columns] = value[:, h * UNIT : (h + 1) * UNIT]

    def gradient(t, h, k, roles):
        slot = lax.rem(partner_s[t, group * 2 + k], 2)
        rows = [window(t, h, role)[slot] for role in roles]
        reals = jnp.concatenate([r[0] for r in rows], axis=0)
        imags = jnp.concatenate([r[1] for r in rows], axis=0)
        sides = jnp.concatenate([reals, imags], axis=1)
        pair = lax.dot_general(own[t, k], sides, NT_DIMS, preferred_element_type=jnp.float32)
        scale = inverse[t, k, h, :, roles[0] * UNIT : (roles[-1] + 1) * UNIT]
        real = (pair[:nv] * scale).astype(jnp.bfloat16)
        imag = (pair[nv:] * scale).astype(jnp.bfloat16)
        mixed = jnp.concatenate(
            [jnp.concatenate([real, -imag], axis=1), jnp.concatenate([imag, real], axis=1)], axis=0
        )
        return jnp.dot(mixed, jnp.concatenate([reals, imags], axis=0), preferred_element_type=jnp.float32)

    def finish(t, k, value):
        out_ref[t, k, 0, 0] = value[:nv].astype(jnp.bfloat16)
        out_ref[t, k, 0, 1] = value[nv:].astype(jnp.bfloat16)

    def unit(t, h):
        for role in (1, 2):
            arrived(t, h, role)

        with scope("unit%d%d" % (t, h)):

            @pl.loop(0, 2)
            def _(k):
                value = gradient(t, h, k, (0, 1, 2))
                if h == 0:
                    total[t, k] = value
                else:
                    finish(t, k, total[t, k] + value)

    late = jnp.logical_not(early)
    late_straight = late & jnp.logical_not(bent)

    @pl.when(early)
    def _():
        for t, c in ((0, 0), (1, 0), (0, 1), (0, 2), (1, 1), (0, 3), (0, 4), (0, 5)):
            take(t, c)
        pl.when(hold)(send_first_transfer)
        take(0, 6, 7, 8)
        take(1, 2, 3)

    @pl.when(late & bent)
    def _():
        take(1, 0, 1, 2)
        take(0, 0, 1)
        take(1, 3)
        take(0, 2, 3)

    @pl.when(late_straight)
    def _():
        take(1, 0)
        pl.when(hold)(send_first_transfer)
        take(1, 1, 2, 3)
        pl.when(jnp.logical_not(hold))(lambda: take(0, 0, 1, 2, 3))

    unit(1, 0)

    @pl.when(late & bent)
    def _():
        take(0, 4, 5, 6, 7, 8)

    @pl.when(late_straight & jnp.logical_not(hold))
    def _():
        take(0, 4)

    unit(1, 1)

    @pl.when(late_straight)
    def _():
        pl.when(hold)(lambda: take(0, 0, 1, 2, 3, 4))
        take(0, 5, 6)

    unit(0, 0)

    @pl.when(late_straight)
    def _():
        take(0, 7, 8)

    unit(0, 1)

    with scope("drain"):
        for copy in (*swaps.values(), *forwards.values()):
            copy.wait_send()


def body(factor, partner, occ_energy, vir_sorted, vir_order):
    transfers, points, _, _, nv, naux = factor.shape
    top_bit = lax.axis_size("kpt").bit_length() - 2
    halves = nv // UNIT
    scratch = [pltpu.VMEM((points, 2, UNIT, naux), jnp.bfloat16)] * (transfers * halves * 3) + [
        pltpu.VMEM((transfers, points, 2 * nv, 2 * naux), jnp.bfloat16),
        pltpu.VMEM((transfers, points, 2 * nv, naux), jnp.float32),
        pltpu.VMEM((transfers, points, halves, nv, 3 * UNIT), jnp.float32),
        pltpu.SMEM(occ_energy.shape, jnp.float32),
        pltpu.SMEM(partner.shape, jnp.int32),
        pltpu.VMEM(vir_sorted.shape, jnp.float32),
        pltpu.VMEM(vir_order.shape, jnp.int32),
        pltpu.SemaphoreType.DMA((3, transfers, MOST)),
        pltpu.SemaphoreType.DMA((3, transfers, MOST)),
        pltpu.SemaphoreType.DMA((transfers, points, 3)),
        pltpu.SemaphoreType.DMA((4,)),
    ]
    return pl.pallas_call(
        functools.partial(kernel, (0, top_bit)),
        out_shape=jax.ShapeDtypeStruct(factor.shape, jnp.bfloat16),
        in_specs=[pl.BlockSpec(memory_space=pltpu.HBM)] * 5,
        out_specs=pl.BlockSpec(memory_space=pltpu.VMEM),
        scratch_shapes=scratch,
        compiler_params=pltpu.CompilerParams(
            collective_id=0, has_side_effects=True, vmem_limit_bytes=40 << 20
        ),
        name="exchange_contract",
    )(*(pltpu.with_memory_space_constraint(x, pltpu.HBM) for x in (factor, partner, occ_energy, vir_sorted, vir_order)))


def solution(mesh):
    in_specs = (P(None, "kpt", "occ", None, None, None), P(), P(), P(), P())
    out_specs = P(None, "kpt", "occ", None, None, None)
    return jax.shard_map(body, mesh=mesh, in_specs=in_specs, out_specs=out_specs, check_vma=False)
```

```python
import functools

import jax
import jax.numpy as jnp
from jax import lax
from jax.experimental import pallas as pl
from jax.experimental.pallas import tpu as pltpu
from jax.sharding import PartitionSpec as P

MESH = pl.DeviceIdType.MESH
scope = jax.named_scope
NT_DIMS = (((1,), (1,)), ((), ()))

UNIT = 128
CHUNKS = (
    ((0, 32), (32, 32), (64, 32), (96, 32), (128, 32), (160, 32), (192, 32), (224, 16), (240, 16)),
    ((0, 64), (64, 64), (128, 64), (192, 64)),
)
MOST = max(len(chunks) for chunks in CHUNKS)


def kernel(flips, factor_ref, partner_ref, occ_ref, sorted_ref, order_ref, out_ref, *scratch):
    nv = factor_ref.shape[4]
    naux = factor_ref.shape[5]
    halves = nv // UNIT
    windows = scratch[: 2 * halves * 3]
    (own, total, inverse, occ_s, partner_s, sorted_v, order_v,
     send_sems, recv_sems, own_sems, table_sems) = scratch[2 * halves * 3 :]
    window = lambda t, h, role: windows[(t * halves + h) * 3 + role]

    group = lax.axis_index("kpt")
    orbit = lax.axis_index("occ")
    orbits = lax.axis_size("occ")
    odd = lax.rem(orbit, 2)
    near = orbit + 1 - 2 * odd
    far = lax.rem(orbit + orbits - 1 + 2 * odd, orbits)
    partners = [(lax.bitwise_xor(group, 1 << flip), orbit) for flip in flips]
    early = lax.rem(group, 2) != orbit // (orbits // 2)
    near_id = (group, near)
    far_id = (group, far)

    tables = [
        pltpu.make_async_copy(src, dst, table_sems.at[n])
        for n, (src, dst) in enumerate(
            ((partner_ref, partner_s), (occ_ref, occ_s), (sorted_ref, sorted_v), (order_ref, order_v))
        )
    ]
    for copy in tables:
        copy.start()
    owns = []
    for t in (1, 0):
        for k in range(2):
            for n, (c, row, col) in enumerate(((0, 0, 0), (1, 0, 1), (1, 1, 0))):
                owns.append(
                    pltpu.make_async_copy(
                        factor_ref.at[t, k, 0, c],
                        own.at[t, k, pl.ds(row * nv, nv), pl.ds(col * naux, naux)],
                        own_sems.at[t, k, n],
                    )
                )
    for copy in owns:
        copy.start()

    half = orbits // 2
    hold = lax.rem(orbit + 2, half) == 0
    bent = orbit // half != far // half
    bent_id = (partners[1][0], far)

    barrier = pltpu.get_barrier_semaphore()
    for target in (*partners, near_id, far_id):
        pl.semaphore_signal(barrier, inc=1, device_id=target, device_id_type=MESH)

    @pl.when(bent)
    def _():
        pl.semaphore_signal(barrier, inc=1, device_id=bent_id, device_id_type=MESH)

    with scope("barrier"):
        pl.semaphore_wait(barrier, 4 + bent.astype(jnp.int32))

    swaps, forwards, straights = {}, {}, {}
    for t in range(2):
        for c, (row, rows) in enumerate(CHUNKS[t]):
            h, at = row // UNIT, row % UNIT
            source = factor_ref.at[t, :, 0, :, pl.ds(row, rows), :]
            here, _, beyond = (window(t, h, role).at[:, :, pl.ds(at, rows), :] for role in range(3))
            swaps[t, c] = pltpu.make_async_remote_copy(
                src_ref=source,
                dst_ref=here,
                send_sem=send_sems.at[0, t, c],
                recv_sem=recv_sems.at[0, t, c],
                device_id=partners[t],
                device_id_type=MESH,
            )
            if t == 1:
                straights[c] = pltpu.make_async_remote_copy(
                    src_ref=source,
                    dst_ref=beyond,
                    send_sem=send_sems.at[2, t, c],
                    recv_sem=recv_sems.at[2, t, c],
                    device_id=bent_id,
                    device_id_type=MESH,
                )
            for role, target in ((2, far_id), (1, near_id)):
                forwards[t, c, role] = pltpu.make_async_remote_copy(
                    src_ref=here,
                    dst_ref=window(t, h, role).at[:, :, pl.ds(at, rows), :],
                    send_sem=send_sems.at[role, t, c],
                    recv_sem=recv_sems.at[role, t, c],
                    device_id=target,
                    device_id_type=MESH,
                )

    slow = lax.rem(orbit + 3, half) == 0
    after = early & (odd == 1) & jnp.logical_not(bent | slow)
    final = len(CHUNKS[0]) - 2

    def send_last_rows():
        for c in range(final, final + 2):
            swaps[0, c].start()

    lead = 3

    def send_lead():
        for c in range(lead):
            swaps[0, c].start()

    def send_rest():
        for c in range(lead, final):
            swaps[0, c].start()
        pl.when(jnp.logical_not(after))(send_last_rows)

    pl.when(jnp.logical_not(hold & early))(send_lead)
    pl.when(jnp.logical_not(hold))(send_rest)
    for c in range(len(CHUNKS[1])):
        pl.when(bent)(straights[c].start)
        swaps[1, c].start()

    def take(t, *chunks):
        for c in chunks:
            with scope("take%d%d" % (t, c)):
                swaps[t, c].wait_recv()
                if t == 1:
                    pl.when(jnp.logical_not(bent))(forwards[t, c, 2].start)
                else:
                    forwards[t, c, 2].start()
                forwards[t, c, 1].start()

    def arrived(t, h, role):
        with scope("arrive%d%d%d" % (t, h, role)):
            for c, (row, _) in enumerate(CHUNKS[t]):
                if row // UNIT == h:
                    forwards[t, c, role].wait_recv()

    for copy in tables:
        copy.wait()
    for copy in owns:
        copy.wait()
    for t in range(2):
        for k in range(2):
            own[t, k, nv:, naux:] = -own[t, k, :nv, :naux]

    lane = lax.broadcasted_iota(jnp.int32, (nv, nv), 1)
    sub = lax.broadcasted_iota(jnp.int32, (nv, nv), 0)
    same = lane == sub

    def as_column(row, zero):
        return jnp.sum(jnp.where(same, row, zero), axis=1, keepdims=True)

    def virtual_row(k):
        ranks = order_v[pl.ds(k, 1), :]
        levels = as_column(sorted_v[pl.ds(k, 1), :], 0.0)
        return jnp.sum(jnp.where(ranks == sub, levels, 0.0), axis=0, keepdims=True)

    roles = (orbit, near, far)
    for k in range(2):
        own_k = group * 2 + k
        own_virtual = virtual_row(own_k)
        own_occ = occ_s[own_k, orbit]
        for t in range(2):
            point = partner_s[t, own_k]
            far_virtual = as_column(virtual_row(point), 0.0)
            for role in range(3):
                pair_occ = own_occ + occ_s[point, roles[role]]
                value = 1.0 / ((pair_occ - far_virtual) - own_virtual)
                for h in range(halves):
                    columns = pl.ds(role * UNIT, UNIT)
                    inverse[t, k, h, :, columns] = value[:, h * UNIT : (h + 1) * UNIT]

    def gradient(t, h, k, roles):
        slot = lax.rem(partner_s[t, group * 2 + k], 2)
        rows = [window(t, h, role)[slot] for role in roles]
        reals = jnp.concatenate([r[0] for r in rows], axis=0)
        imags = jnp.concatenate([r[1] for r in rows], axis=0)
        sides = jnp.concatenate([reals, imags], axis=1)
        pair = lax.dot_general(own[t, k], sides, NT_DIMS, preferred_element_type=jnp.float32)
        scale = inverse[t, k, h, :, roles[0] * UNIT : (roles[-1] + 1) * UNIT]
        real = (pair[:nv] * scale).astype(jnp.bfloat16)
        imag = (pair[nv:] * scale).astype(jnp.bfloat16)
        mixed = jnp.concatenate(
            [jnp.concatenate([real, -imag], axis=1), jnp.concatenate([imag, real], axis=1)], axis=0
        )
        return jnp.dot(mixed, jnp.concatenate([reals, imags], axis=0), preferred_element_type=jnp.float32)

    def finish(t, k, value):
        out_ref[t, k, 0, 0] = value[:nv].astype(jnp.bfloat16)
        out_ref[t, k, 0, 1] = value[nv:].astype(jnp.bfloat16)

    def unit(t, h):
        for role in (1, 2):
            arrived(t, h, role)

        with scope("unit%d%d" % (t, h)):

            @pl.loop(0, 2, unroll=(t, h) == (0, 1))
            def _(k):
                value = gradient(t, h, k, (0, 1, 2))
                if h == 0:
                    total[t, k] = value
                else:
                    finish(t, k, total[t, k] + value)

    late = jnp.logical_not(early)
    plain = late & jnp.logical_not(bent | hold | slow)

    @pl.when(early & jnp.logical_not(hold))
    def _():
        for t, c in ((0, 0), (1, 0), (0, 1), (0, 2), (1, 1), (0, 3), (0, 4), (0, 5)):
            take(t, c)
        take(0, 6, 7, 8)
        take(1, 2, 3)

    @pl.when(early & hold)
    def _():
        for t, c in ((1, 0), (1, 1), (0, 0), (0, 1), (0, 2), (1, 2)):
            take(t, c)
        send_lead()
        send_rest()
        take(0, 3)
        take(1, 3)
        take(0, 4, 5, 6, 7, 8)

    @pl.when(late & bent)
    def _():
        for t, c in ((1, 0), (0, 0), (0, 1), (1, 1), (0, 2), (0, 3), (1, 2), (0, 4), (0, 5), (1, 3)):
            take(t, c)

    @pl.when(late & jnp.logical_not(bent))
    def _():
        take(1, 0)
        pl.when(hold)(send_rest)
        take(1, 1, 2, 3)
        take(0, 0, 1)
        pl.when(jnp.logical_not(hold))(lambda: take(0, 2, 3))

    unit(1, 0)

    pl.when(late & slow)(lambda: take(0, 4, 5))
    pl.when(late & (bent | slow))(lambda: take(0, 6, 7, 8))
    pl.when(late & hold)(lambda: take(0, 2, 3))
    pl.when(late & jnp.logical_not(bent | slow))(lambda: take(0, 4))

    unit(1, 1)

    pl.when(late & hold)(lambda: take(0, 5, 6, 7, 8))
    pl.when(plain)(lambda: take(0, 5))

    unit(0, 0)

    pl.when(plain)(lambda: take(0, 6, 7, 8))

    unit(0, 1)

    with scope("drain"):
        swaps[0, final - 1].wait_send()
        pl.when(after)(send_last_rows)
        for at, copy in (*swaps.items(), *forwards.items()):
            if at != (0, final - 1):
                copy.wait_send()


def body(factor, partner, occ_energy, vir_sorted, vir_order):
    transfers, points, _, _, nv, naux = factor.shape
    top_bit = lax.axis_size("kpt").bit_length() - 2
    halves = nv // UNIT
    scratch = [pltpu.VMEM((points, 2, UNIT, naux), jnp.bfloat16)] * (transfers * halves * 3) + [
        pltpu.VMEM((transfers, points, 2 * nv, 2 * naux), jnp.bfloat16),
        pltpu.VMEM((transfers, points, 2 * nv, naux), jnp.float32),
        pltpu.VMEM((transfers, points, halves, nv, 3 * UNIT), jnp.float32),
        pltpu.SMEM(occ_energy.shape, jnp.float32),
        pltpu.SMEM(partner.shape, jnp.int32),
        pltpu.VMEM(vir_sorted.shape, jnp.float32),
        pltpu.VMEM(vir_order.shape, jnp.int32),
        pltpu.SemaphoreType.DMA((3, transfers, MOST)),
        pltpu.SemaphoreType.DMA((3, transfers, MOST)),
        pltpu.SemaphoreType.DMA((transfers, points, 3)),
        pltpu.SemaphoreType.DMA((4,)),
    ]
    return pl.pallas_call(
        functools.partial(kernel, (0, top_bit)),
        out_shape=jax.ShapeDtypeStruct(factor.shape, jnp.bfloat16),
        in_specs=[pl.BlockSpec(memory_space=pltpu.HBM)] * 5,
        out_specs=pl.BlockSpec(memory_space=pltpu.VMEM),
        scratch_shapes=scratch,
        compiler_params=pltpu.CompilerParams(
            collective_id=0, has_side_effects=True, vmem_limit_bytes=40 << 20
        ),
        name="exchange_contract",
    )(*(pltpu.with_memory_space_constraint(x, pltpu.HBM) for x in (factor, partner, occ_energy, vir_sorted, vir_order)))


def solution(mesh):
    in_specs = (P(None, "kpt", "occ", None, None, None), P(), P(), P(), P())
    out_specs = P(None, "kpt", "occ", None, None, None)
    return jax.shard_map(body, mesh=mesh, in_specs=in_specs, out_specs=out_specs, check_vma=False)
```

```python
import functools

import jax
import jax.numpy as jnp
from jax import lax
from jax.experimental import pallas as pl
from jax.experimental.pallas import tpu as pltpu
from jax.sharding import PartitionSpec as P

MESH = pl.DeviceIdType.MESH
scope = jax.named_scope
NT_DIMS = (((1,), (1,)), ((), ()))

UNIT = 128
CHUNKS = (
    ((0, 32), (32, 32), (64, 32), (96, 32), (128, 32), (160, 32), (192, 32), (224, 16), (240, 16)),
    ((0, 64), (64, 64), (128, 64), (192, 64)),
)
MOST = max(len(chunks) for chunks in CHUNKS)


def kernel(flips, factor_ref, partner_ref, occ_ref, sorted_ref, order_ref, out_ref, *scratch):
    nv = factor_ref.shape[4]
    naux = factor_ref.shape[5]
    halves = nv // UNIT
    windows = scratch[: 2 * halves * 3]
    (own, total, inverse, occ_s, partner_s, sorted_v, order_v,
     send_sems, recv_sems, own_sems, table_sems) = scratch[2 * halves * 3 :]
    window = lambda t, h, role: windows[(t * halves + h) * 3 + role]

    group = lax.axis_index("kpt")
    orbit = lax.axis_index("occ")
    orbits = lax.axis_size("occ")
    odd = lax.rem(orbit, 2)
    near = orbit + 1 - 2 * odd
    far = lax.rem(orbit + orbits - 1 + 2 * odd, orbits)
    partners = [(lax.bitwise_xor(group, 1 << flip), orbit) for flip in flips]
    early = lax.rem(group, 2) != orbit // (orbits // 2)
    near_id = (group, near)
    far_id = (group, far)

    tables = [
        pltpu.make_async_copy(src, dst, table_sems.at[n])
        for n, (src, dst) in enumerate(
            ((partner_ref, partner_s), (occ_ref, occ_s), (sorted_ref, sorted_v), (order_ref, order_v))
        )
    ]
    for copy in tables:
        copy.start()
    owns = []
    for t in (1, 0):
        for k in range(2):
            for n, (c, row, col) in enumerate(((0, 0, 0), (1, 0, 1), (1, 1, 0))):
                owns.append(
                    pltpu.make_async_copy(
                        factor_ref.at[t, k, 0, c],
                        own.at[t, k, pl.ds(row * nv, nv), pl.ds(col * naux, naux)],
                        own_sems.at[t, k, n],
                    )
                )
    for copy in owns:
        copy.start()

    half = orbits // 2
    hold = lax.rem(orbit + 2, half) == 0
    bent = orbit // half != far // half
    bent_id = (partners[1][0], far)

    barrier = pltpu.get_barrier_semaphore()
    for target in (*partners, near_id, far_id):
        pl.semaphore_signal(barrier, inc=1, device_id=target, device_id_type=MESH)

    @pl.when(bent)
    def _():
        pl.semaphore_signal(barrier, inc=1, device_id=bent_id, device_id_type=MESH)

    with scope("barrier"):
        pl.semaphore_wait(barrier, 4 + bent.astype(jnp.int32))

    swaps, forwards, straights = {}, {}, {}
    for t in range(2):
        for c, (row, rows) in enumerate(CHUNKS[t]):
            h, at = row // UNIT, row % UNIT
            source = factor_ref.at[t, :, 0, :, pl.ds(row, rows), :]
            here, _, beyond = (window(t, h, role).at[:, :, pl.ds(at, rows), :] for role in range(3))
            swaps[t, c] = pltpu.make_async_remote_copy(
                src_ref=source,
                dst_ref=here,
                send_sem=send_sems.at[0, t, c],
                recv_sem=recv_sems.at[0, t, c],
                device_id=partners[t],
                device_id_type=MESH,
            )
            if t == 1:
                straights[c] = pltpu.make_async_remote_copy(
                    src_ref=source,
                    dst_ref=beyond,
                    send_sem=send_sems.at[2, t, c],
                    recv_sem=recv_sems.at[2, t, c],
                    device_id=bent_id,
                    device_id_type=MESH,
                )
            for role, target in ((2, far_id), (1, near_id)):
                forwards[t, c, role] = pltpu.make_async_remote_copy(
                    src_ref=here,
                    dst_ref=window(t, h, role).at[:, :, pl.ds(at, rows), :],
                    send_sem=send_sems.at[role, t, c],
                    recv_sem=recv_sems.at[role, t, c],
                    device_id=target,
                    device_id_type=MESH,
                )

    slow = lax.rem(orbit + 3, half) == 0
    after = early & (odd == 1) & jnp.logical_not(bent | slow)
    final = len(CHUNKS[0]) - 3

    def send_last_rows():
        for c in range(final, final + 3):
            swaps[0, c].start()

    lead = 3

    def send_lead():
        for c in range(lead):
            swaps[0, c].start()

    def send_rest():
        for c in range(lead, final):
            swaps[0, c].start()
        pl.when(jnp.logical_not(after))(send_last_rows)

    pl.when(jnp.logical_not(hold & early))(send_lead)
    pl.when(jnp.logical_not(hold))(send_rest)
    for c in range(len(CHUNKS[1])):
        pl.when(bent)(straights[c].start)
        swaps[1, c].start()

    def take(t, *chunks):
        for c in chunks:
            with scope("take%d%d" % (t, c)):
                swaps[t, c].wait_recv()
                if t == 1:
                    pl.when(jnp.logical_not(bent))(forwards[t, c, 2].start)
                else:
                    forwards[t, c, 2].start()
                forwards[t, c, 1].start()

    def arrived(t, h, role):
        with scope("arrive%d%d%d" % (t, h, role)):
            for c, (row, _) in enumerate(CHUNKS[t]):
                if row // UNIT == h:
                    forwards[t, c, role].wait_recv()

    for copy in tables:
        copy.wait()
    for copy in owns:
        copy.wait()
    for t in range(2):
        for k in range(2):
            own[t, k, nv:, naux:] = -own[t, k, :nv, :naux]

    lane = lax.broadcasted_iota(jnp.int32, (nv, nv), 1)
    sub = lax.broadcasted_iota(jnp.int32, (nv, nv), 0)
    same = lane == sub

    def as_column(row, zero):
        return jnp.sum(jnp.where(same, row, zero), axis=1, keepdims=True)

    def virtual_row(k):
        ranks = order_v[pl.ds(k, 1), :]
        levels = as_column(sorted_v[pl.ds(k, 1), :], 0.0)
        return jnp.sum(jnp.where(ranks == sub, levels, 0.0), axis=0, keepdims=True)

    roles = (orbit, near, far)
    for k in range(2):
        own_k = group * 2 + k
        own_virtual = virtual_row(own_k)
        own_occ = occ_s[own_k, orbit]
        for t in range(2):
            point = partner_s[t, own_k]
            far_virtual = as_column(virtual_row(point), 0.0)
            for role in range(3):
                pair_occ = own_occ + occ_s[point, roles[role]]
                value = 1.0 / ((pair_occ - far_virtual) - own_virtual)
                for h in range(halves):
                    columns = pl.ds(role * UNIT, UNIT)
                    inverse[t, k, h, :, columns] = value[:, h * UNIT : (h + 1) * UNIT]

    def gradient(t, h, k, roles):
        slot = lax.rem(partner_s[t, group * 2 + k], 2)
        rows = [window(t, h, role)[slot] for role in roles]
        reals = jnp.concatenate([r[0] for r in rows], axis=0)
        imags = jnp.concatenate([r[1] for r in rows], axis=0)
        sides = jnp.concatenate([reals, imags], axis=1)
        pair = lax.dot_general(own[t, k], sides, NT_DIMS, preferred_element_type=jnp.float32)
        scale = inverse[t, k, h, :, roles[0] * UNIT : (roles[-1] + 1) * UNIT]
        real = (pair[:nv] * scale).astype(jnp.bfloat16)
        imag = (pair[nv:] * scale).astype(jnp.bfloat16)
        mixed = jnp.concatenate(
            [jnp.concatenate([real, -imag], axis=1), jnp.concatenate([imag, real], axis=1)], axis=0
        )
        return jnp.dot(mixed, jnp.concatenate([reals, imags], axis=0), preferred_element_type=jnp.float32)

    def finish(t, k, value):
        out_ref[t, k, 0, 0] = value[:nv].astype(jnp.bfloat16)
        out_ref[t, k, 0, 1] = value[nv:].astype(jnp.bfloat16)

    def unit(t, h):
        for role in (1, 2):
            arrived(t, h, role)

        with scope("unit%d%d" % (t, h)):

            @pl.loop(0, 2, unroll=(t, h) == (0, 1))
            def _(k):
                value = gradient(t, h, k, (0, 1, 2))
                if h == 0:
                    total[t, k] = value
                else:
                    finish(t, k, total[t, k] + value)

    late = jnp.logical_not(early)
    plain = late & jnp.logical_not(bent | hold | slow)

    @pl.when(early & jnp.logical_not(hold))
    def _():
        for t, c in ((0, 0), (1, 0), (0, 1), (0, 2), (1, 1), (0, 3), (0, 4), (0, 5)):
            take(t, c)
        take(0, 6, 7, 8)
        take(1, 2, 3)

    @pl.when(early & hold)
    def _():
        for t, c in ((1, 0), (1, 1), (0, 0), (0, 1), (0, 2), (1, 2)):
            take(t, c)
        send_lead()
        send_rest()
        take(0, 3)
        take(1, 3)
        take(0, 4, 5, 6, 7, 8)

    @pl.when(late & bent)
    def _():
        for t, c in ((1, 0), (0, 0), (0, 1), (1, 1), (0, 2), (0, 3), (1, 2), (0, 4), (0, 5)):
            take(t, c)
        pl.when(odd == 1)(lambda: take(0, 6, 7, 8))
        take(1, 3)

    @pl.when(late & jnp.logical_not(bent))
    def _():
        take(1, 0)
        pl.when(hold)(send_rest)
        take(1, 1, 2, 3)
        take(0, 0, 1)
        pl.when(jnp.logical_not(hold))(lambda: take(0, 2, 3))

    unit(1, 0)

    pl.when(late & slow)(lambda: take(0, 4, 5))
    pl.when(late & (bent & (odd == 0) | slow))(lambda: take(0, 6, 7, 8))
    pl.when(late & hold)(lambda: take(0, 2, 3))
    pl.when(late & jnp.logical_not(bent | slow))(lambda: take(0, 4))

    unit(1, 1)

    pl.when(late & hold)(lambda: take(0, 5, 6, 7, 8))
    pl.when(plain)(lambda: take(0, 5))
    pl.when(plain & (odd == 0))(lambda: take(0, 6, 7, 8))

    unit(0, 0)

    pl.when(plain & (odd == 1))(lambda: take(0, 6, 7, 8))

    unit(0, 1)

    with scope("drain"):
        swaps[0, final - 1].wait_send()
        pl.when(after)(send_last_rows)
        for at, copy in (*swaps.items(), *forwards.items()):
            if at != (0, final - 1):
                copy.wait_send()


def body(factor, partner, occ_energy, vir_sorted, vir_order):
    transfers, points, _, _, nv, naux = factor.shape
    top_bit = lax.axis_size("kpt").bit_length() - 2
    halves = nv // UNIT
    scratch = [pltpu.VMEM((points, 2, UNIT, naux), jnp.bfloat16)] * (transfers * halves * 3) + [
        pltpu.VMEM((transfers, points, 2 * nv, 2 * naux), jnp.bfloat16),
        pltpu.VMEM((transfers, points, 2 * nv, naux), jnp.float32),
        pltpu.VMEM((transfers, points, halves, nv, 3 * UNIT), jnp.float32),
        pltpu.SMEM(occ_energy.shape, jnp.float32),
        pltpu.SMEM(partner.shape, jnp.int32),
        pltpu.VMEM(vir_sorted.shape, jnp.float32),
        pltpu.VMEM(vir_order.shape, jnp.int32),
        pltpu.SemaphoreType.DMA((3, transfers, MOST)),
        pltpu.SemaphoreType.DMA((3, transfers, MOST)),
        pltpu.SemaphoreType.DMA((transfers, points, 3)),
        pltpu.SemaphoreType.DMA((4,)),
    ]
    return pl.pallas_call(
        functools.partial(kernel, (0, top_bit)),
        out_shape=jax.ShapeDtypeStruct(factor.shape, jnp.bfloat16),
        in_specs=[pl.BlockSpec(memory_space=pltpu.HBM)] * 5,
        out_specs=pl.BlockSpec(memory_space=pltpu.VMEM),
        scratch_shapes=scratch,
        compiler_params=pltpu.CompilerParams(
            collective_id=0, has_side_effects=True, vmem_limit_bytes=40 << 20
        ),
        name="exchange_contract",
    )(*(pltpu.with_memory_space_constraint(x, pltpu.HBM) for x in (factor, partner, occ_energy, vir_sorted, vir_order)))


def solution(mesh):
    in_specs = (P(None, "kpt", "occ", None, None, None), P(), P(), P(), P())
    out_specs = P(None, "kpt", "occ", None, None, None)
    return jax.shard_map(body, mesh=mesh, in_specs=in_specs, out_specs=out_specs, check_vma=False)
```
